32 devices in a mesh: inner: 2 (over core), outer: 16 (over z, y, x).
Axes of the slice: x: 2, y: 2, z: 4, core: 2. Of those that a mesh axis runs over, the one named last changes fastest.
Arguments:
- images: bfloat16 [32, 4, 256, 1152], P(('inner', 'outer')), may hold values from -6 to 6
- counts: int32 [32], P(('inner', 'outer')), may hold values from 1 to 4, as said below
- ln1_gain: bfloat16 [1152], P('inner'), may hold values from 0.5 to 1.5
- ln1_bias: bfloat16 [1152], P('inner'), may hold values from -1.75 to 1.75
- w_qkv: bfloat16 [1152, 3456], P('inner'), may hold values from -0.1875 to 0.1875
- b_qv: bfloat16 [2304], P('inner'), may hold values from -3 to 3
- w_attn_out: bfloat16 [1152, 1152], P('inner'), may hold values from -0.75 to 0.75
- b_attn_out: bfloat16 [1152], P('inner'), may hold values from -1.75 to 1.75
- ln2_gain: bfloat16 [1152], P('inner'), may hold values from 0.5 to 1.5
- ln2_bias: bfloat16 [1152], P('inner'), may hold values from -1.75 to 1.75
- w_mlp_in: bfloat16 [1152, 4304], P('inner'), may hold values from -0.1875 to 0.1875
- b_mlp_in: bfloat16 [4304], P('inner'), may hold values from -3 to 3
- w_mlp_out: bfloat16 [4304, 1152], P('inner'), may hold values from -0.09375 to 0.09375
- b_mlp_out: bfloat16 [1152], P('inner'), may hold values from -1.75 to 1.75
- cotangent: bfloat16 [32, 4, 256, 1152], P(('inner', 'outer')), may hold values from -6 to 6
Outputs:
- block_out: bfloat16 [32, 4, 256, 1152], P(('inner', 'outer'))
- grad_images: bfloat16 [32, 4, 256, 1152], P(('inner', 'outer'))
- grad_ln1_gain: float32 [1152], P('inner')
- grad_ln1_bias: float32 [1152], P('inner')
- grad_w_qkv: float32 [1152, 3456], P('inner')
- grad_b_qv: float32 [2304], P('inner')
- grad_w_attn_out: float32 [1152, 1152], P('inner')
- grad_b_attn_out: float32 [1152], P('inner')
- grad_ln2_gain: float32 [1152], P('inner')
- grad_ln2_bias: float32 [1152], P('inner')
- grad_w_mlp_in: float32 [1152, 4304], P('inner')
- grad_b_mlp_in: float32 [4304], P('inner')
- grad_w_mlp_out: float32 [4304, 1152], P('inner')
- grad_b_mlp_out: float32 [1152], P('inner')
The draws below stay inside these ranges and needn't reach their ends.
Inputs may be any that keep to these rules, and one draw needn't show every extreme that they name: `counts`: each device's images fill its slots from the first one on; some device holds 4.
All inputs are finite; a program needn't handle non-finite values.
Results may differ from the reference program's by a relative error of at most 0.013.
Values may be sent and summed in bfloat16 or wider, within the bound.
No kernel may reach another device: no remote copies, remote signals or barrier semaphores. Data moves between devices by JAX's collectives and lax.ppermute only.
A program may use at most 320 MiB of HBM per device.

```python
import math
import jax
import jax.numpy as jnp
from jax import lax

D = 1152
HEADS = 16
HEAD_DIM = 72
FF = 4304
IMG_TOK = 256
MICRO = 2
SLOTS = 2
DEVICES = 32


def draw_counts(key, part):
    held = jax.random.randint(key, (DEVICES,), 1, MICRO * SLOTS + 1)
    fullest = jax.random.randint(jax.random.fold_in(key, 7), (), 0, DEVICES)
    return jnp.where(jnp.arange(DEVICES) == fullest, MICRO * SLOTS, held).astype(jnp.int32)


def level_of(stream_key, dims, shards, smallest, high):
    loudness, own = 1.0, jax.random.fold_in(stream_key, 6)
    for axis_at, parts in shards:
        heights = jnp.exp(jax.random.uniform(jax.random.fold_in(own, axis_at), (parts,), jnp.float32, smallest / len(shards), high / len(shards)))
        loudness = loudness * jnp.repeat(heights, dims[axis_at] // parts).reshape([-1 if axis == axis_at else 1 for axis in range(len(dims))])
    return loudness


def normal_values(key, extent, deviation, reach, shards=(), held_as=jnp.bfloat16):
    array = deviation * jax.random.normal(key, extent, jnp.float32)
    if shards:
        array = array * level_of(key, extent, shards, -0.22, 0.18)
    return jnp.clip(array, -reach, reach).astype(held_as)


def setup_inputs(seed: int = 0) -> dict:
    keys = jax.random.split(jax.random.key(seed), 16)
    images = normal_values(keys[0], (DEVICES, MICRO * SLOTS, IMG_TOK, D), 1.0, 6.0, ((0, 32),))
    counts = draw_counts(jax.random.fold_in(keys[15], 71), 0)
    ln1_gain = jnp.clip(1.0 + 0.1 * jax.random.normal(keys[2], (D,), jnp.float32), 0.5, 1.5).astype(jnp.bfloat16)
    ln1_bias = normal_values(keys[3], (D,), 0.3, 1.75, ((0, 2),))
    w_qkv = normal_values(keys[4], (D, 3 * D), D ** -0.5, 0.1875, ((0, 2),))
    b_qv = normal_values(keys[5], (2 * D,), 0.5, 3.0, ((0, 2),))
    w_attn_out = normal_values(keys[6], (D, D), (D // 16) ** -0.5, 0.75, ((0, 2),))
    b_attn_out = normal_values(keys[7], (D,), 0.3, 1.75, ((0, 2),))
    ln2_gain = jnp.clip(1.0 + 0.1 * jax.random.normal(keys[8], (D,), jnp.float32), 0.5, 1.5).astype(jnp.bfloat16)
    ln2_bias = normal_values(keys[9], (D,), 0.3, 1.75, ((0, 2),))
    w_mlp_in = normal_values(keys[10], (D, FF), D ** -0.5, 0.1875, ((0, 2),))
    b_mlp_in = normal_values(keys[11], (FF,), 0.5, 3.0, ((0, 2),))
    w_mlp_out = normal_values(keys[12], (FF, D), FF ** -0.5, 0.09375, ((0, 2),))
    b_mlp_out = normal_values(keys[13], (D,), 0.3, 1.75, ((0, 2),))
    cotangent = normal_values(keys[14], (DEVICES, MICRO * SLOTS, IMG_TOK, D), 1.0, 6.0, ((0, 32),))
    return dict(images=images, counts=counts, ln1_gain=ln1_gain, ln1_bias=ln1_bias, w_qkv=w_qkv, b_qv=b_qv, w_attn_out=w_attn_out, b_attn_out=b_attn_out, ln2_gain=ln2_gain, ln2_bias=ln2_bias, w_mlp_in=w_mlp_in, b_mlp_in=b_mlp_in, w_mlp_out=w_mlp_out, b_mlp_out=b_mlp_out, cotangent=cotangent)


@jax.custom_vjp
def low(v):
    return lax.optimization_barrier(v.astype(jnp.bfloat16)).astype(jnp.float32)

@jax.custom_vjp
def low_back(v):
    return v

def low_keep(v):
    return (low(v), None)

def low_pass(kept, grad):
    return (grad,)

def back_keep(v):
    return (v, None)

def back_low(kept, grad):
    return (low(grad),)
low.defvjp(low_keep, low_pass)
low_back.defvjp(back_keep, back_low)
highest = lax.Precision.HIGHEST

def norm_rows(rows, gain, shift):
    mean_row = lax.optimization_barrier(jnp.mean(rows, -1, keepdims=True))
    centered = rows - mean_row
    variance = lax.optimization_barrier(jnp.mean(centered * centered, -1, keepdims=True))
    return centered * lax.rsqrt(variance + 1e-06) * gain + shift

def block_forward(weights, group_rows):
    ln1_gain, ln1_bias, w_qkv, b_qv, w_attn_out, b_attn_out, ln2_gain, ln2_bias, w_mlp_in, b_mlp_in, w_mlp_out, b_mlp_out = weights
    group_count, length, model_width = group_rows.shape
    score_scale = 1.0 / math.sqrt(HEAD_DIM)
    normed_one = low(norm_rows(group_rows, ln1_gain, ln1_bias))
    projected = jnp.einsum('gtd,de->gte', normed_one, w_qkv, precision=highest)
    queries = low(low_back(projected[..., :model_width] + b_qv[:model_width]))
    key_rows = low(low_back(projected[..., model_width:2 * model_width]))
    value_rows = low(low_back(projected[..., 2 * model_width:] + b_qv[model_width:]))

    def split_heads(tensor):
        return tensor.reshape(group_count, length, HEADS, HEAD_DIM)
    scores = low_back(jnp.einsum('gqhd,gkhd->ghqk', split_heads(queries), split_heads(key_rows), precision=highest) * score_scale)
    attn_probs = jax.nn.softmax(scores, axis=-1)
    attended = jnp.einsum('ghqk,gkhd->gqhd', low(attn_probs), split_heads(value_rows), precision=highest)
    attended = low(low_back(attended.reshape(group_count, length, model_width)))
    branch = low_back(jnp.einsum('gtd,de->gte', attended, w_attn_out, precision=highest) + b_attn_out)
    hidden = group_rows + branch
    normed_two = low(norm_rows(hidden, ln2_gain, ln2_bias))
    pre_act = low_back(jnp.einsum('gtd,df->gtf', normed_two, w_mlp_in, precision=highest) + b_mlp_in)
    activated = low(jax.nn.gelu(pre_act, approximate=True))
    second = low_back(jnp.einsum('gtf,fd->gtd', activated, w_mlp_out, precision=highest) + b_mlp_out)
    return hidden + second

def reference(images, counts, ln1_gain, ln1_bias, w_qkv, b_qv, w_attn_out, b_attn_out, ln2_gain, ln2_bias, w_mlp_in, b_mlp_in, w_mlp_out, b_mlp_out, cotangent):
    devices, slots, length, model_width = images.shape
    total = devices * slots
    per_group = math.gcd(total, max(1, 4096 // length))
    groups = total // per_group
    live = (jnp.arange(slots, dtype=jnp.int32)[None, :] < counts[:, None]).astype(jnp.float32)
    live_rows = live.reshape(groups, per_group, 1, 1)
    flat = images.astype(jnp.float32).reshape(groups, per_group, length, model_width)
    weights = tuple((w.astype(jnp.float32) for w in (ln1_gain, ln1_bias, w_qkv, b_qv, w_attn_out, b_attn_out, ln2_gain, ln2_bias, w_mlp_in, b_mlp_in, w_mlp_out, b_mlp_out)))

    def forward(weights, flat):
        step_fn = jax.checkpoint(lambda rows: block_forward(weights, rows))
        return lax.map(step_fn, flat)
    outputs, pullback = jax.vjp(forward, weights, flat)
    masked_cot = cotangent.astype(jnp.float32).reshape(groups, per_group, length, model_width) * live_rows
    weight_grads, input_grad = pullback(masked_cot)
    block_out = (outputs * live_rows).reshape(images.shape).astype(jnp.bfloat16)
    grad_images = input_grad.reshape(images.shape).astype(jnp.bfloat16)
    return (block_out, grad_images, weight_grads[0], weight_grads[1], weight_grads[2], weight_grads[3], weight_grads[4], weight_grads[5], weight_grads[6], weight_grads[7], weight_grads[8], weight_grads[9], weight_grads[10], weight_grads[11])
```

```python
import functools
import math

import jax
import jax.numpy as jnp
from jax import lax
from jax.sharding import PartitionSpec as P

HEADS = 16
HEAD_DIM = 72


epsilon = 1e-06
tanh_coef = 0.7978845608028654
cubic_coef = 0.044715


def norm_parts(rows, gain, shift):
    mean_row = jnp.mean(rows, -1, keepdims=True)
    centered = rows - mean_row
    inv_std = lax.rsqrt(jnp.mean(centered * centered, -1, keepdims=True) + epsilon)
    unit_rows = centered * inv_std
    return (unit_rows * gain + shift, unit_rows, inv_std)


def norm_back(grad_normed, unit_rows, inv_std, gain):
    grad_unit = grad_normed * gain
    return inv_std * (
        grad_unit
        - jnp.mean(grad_unit, -1, keepdims=True)
        - unit_rows * jnp.mean(grad_unit * unit_rows, -1, keepdims=True)
    )


def gelu_parts(pre_act):
    tangent = jnp.tanh(tanh_coef * (pre_act + cubic_coef * pre_act * pre_act * pre_act))
    activated = 0.5 * pre_act * (1.0 + tangent)
    derivative = 0.5 * (1.0 + tangent) + 0.5 * pre_act * (1.0 - tangent * tangent) * tanh_coef * (
        1.0 + 3.0 * cubic_coef * pre_act * pre_act
    )
    return (activated, derivative)


def matmul(left, right):
    return jnp.dot(left, right, preferred_element_type=jnp.float32)


def outer_sum(left, right):
    return lax.dot_general(
        left, right, (((0,), (0,)), ((), ())), preferred_element_type=jnp.float32
    )


def times_rows(left, right):
    return lax.dot_general(
        left, right, (((1,), (1,)), ((), ())), preferred_element_type=jnp.float32
    )


def cut(tensor, at, size):
    return lax.dynamic_slice_in_dim(tensor, at * size, size, 0)


def swap(tensor, axis, size, stride):
    return lax.ppermute(tensor, axis, [(i, i ^ stride) for i in range(size)])


def bit_of(axis, stride):
    return (lax.axis_index(axis) // stride) % 2


def pad_rows(tensor, rows):
    return tensor if tensor.shape[0] == rows else jnp.pad(tensor, ((0, rows - tensor.shape[0]), (0, 0)))


def scatter_stage(total, axis, size, stride):
    rows = -(-total.shape[0] // 16) * 16
    total = pad_rows(total, rows)
    bit = bit_of(axis, stride)
    arrived = swap(cut(total, 1 - bit, rows // 2).astype(jnp.bfloat16), axis, size, stride)
    return cut(total, bit, rows // 2) + arrived.astype(jnp.float32)


def join(own, other, bit):
    return jnp.where(bit == 0, jnp.concatenate([own, other], 0), jnp.concatenate([other, own], 0))


def gather_stage(block, axis, size, stride):
    return join(block, swap(block, axis, size, stride), bit_of(axis, stride))


def reduce_outer(total, size, order):
    if size & (size - 1):
        return lax.psum(total, "outer")
    shapes = []
    for stride in order:
        shapes.append(total.shape[0])
        total = scatter_stage(total, "outer", size, stride)
    block = total.astype(jnp.bfloat16)
    for stride, rows in zip(reversed(order), reversed(shapes)):
        block = gather_stage(block, "outer", size, stride)[:rows]
    return block.astype(jnp.float32)


def orders(size):
    strides = [1 << k for k in range(size.bit_length() - 1)]
    other = strides[1:2] + strides[:1] + strides[2:]
    return strides, other


def sum_to_owner(grad, inner, outer):
    rows = grad.shape[0] // inner
    if inner == 2:
        bit = lax.axis_index("inner")
        arrived = swap(cut(grad, 1 - bit, rows).astype(jnp.bfloat16), "inner", 2, 1)
        mine = cut(grad, bit, rows) + arrived.astype(jnp.float32)
    else:
        mine = lax.psum_scatter(grad, "inner", scatter_dimension=0, tiled=True)
    first, second = orders(outer)
    middle = (grad.shape[1] // 256) * 128
    return jnp.concatenate(
        [
            reduce_outer(mine[:, :middle], outer, first),
            reduce_outer(mine[:, middle:], outer, second),
        ],
        1,
    )


def sum_everywhere(vector, inner, outer):
    for axis, size in (("inner", inner), ("outer", outer)):
        if size & (size - 1):
            vector = lax.psum(vector, axis)
        else:
            stride = 1
            while stride < size:
                vector = vector + swap(vector, axis, size, stride)
                stride *= 2
    return vector


def whole(shard, inner):
    if inner == 2:
        return join(shard, swap(shard, "inner", 2, 1), lax.axis_index("inner"))
    return lax.all_gather(shard, "inner", axis=0, tiled=True)


def swap_small(small, shards, inner):
    if inner == 2:
        other = swap(small.reshape(1, -1), "inner", 2, 1).reshape(-1)
    every = lax.all_gather(small, "inner") if inner != 2 else None
    out = {}
    at = 0
    for k in (0, 1, 3, 5, 6, 7, 9, 11):
        size = shards[k].shape[0]
        if inner == 2:
            out[k] = join(small[at : at + size], other[at : at + size], lax.axis_index("inner"))
        else:
            out[k] = every[:, at : at + size].reshape(-1)
        at += size
    return out


def per_device(
    inner,
    outer,
    images,
    counts,
    ln1_gain,
    ln1_bias,
    w_qkv,
    b_qv,
    w_attn_out,
    b_attn_out,
    ln2_gain,
    ln2_bias,
    w_mlp_in,
    b_mlp_in,
    w_mlp_out,
    b_mlp_out,
    cotangent,
):
    shards = (
        ln1_gain,
        ln1_bias,
        w_qkv,
        b_qv,
        w_attn_out,
        b_attn_out,
        ln2_gain,
        ln2_bias,
        w_mlp_in,
        b_mlp_in,
        w_mlp_out,
        b_mlp_out,
    )
    slot_count = images.shape[1]
    length = images.shape[2]
    model_width = images.shape[3]
    rows = slot_count * length
    score_scale = 1.0 / math.sqrt(HEAD_DIM)

    def split_heads(tensor):
        return tensor.reshape(slot_count, length, HEADS, HEAD_DIM)

    small = jnp.concatenate([shards[k] for k in (0, 1, 3, 5, 6, 7, 9, 11)])
    small = swap_small(small, shards, inner)
    full = tuple(
        small[k] if k in small else whole(shards[k], inner) for k in range(12)
    )
    gain_one = full[0].astype(jnp.float32)
    shift_one = full[1].astype(jnp.float32)
    whole_qkv = full[2]
    qv_bias = full[3].astype(jnp.float32)
    whole_attn = full[4]
    bias_attn = full[5].astype(jnp.float32)
    gain_two = full[6].astype(jnp.float32)
    shift_two = full[7].astype(jnp.float32)
    whole_up = full[8]
    bias_up = full[9].astype(jnp.float32)
    whole_down = full[10]
    bias_down = full[11].astype(jnp.float32)
    start = 0
    source = (
        images[0, start : start + slot_count].reshape(rows, model_width).astype(jnp.float32)
    )
    slot_ids = start + jnp.arange(slot_count, dtype=jnp.int32)
    live = (slot_ids < counts[0]).astype(jnp.float32)
    live_rows = jnp.repeat(live, length)[:, None]
    normed_one, unit_one, inv_one = norm_parts(source, gain_one, shift_one)
    normed_low = normed_one.astype(jnp.bfloat16)
    projected = matmul(normed_low, whole_qkv)
    queries = (projected[:, :model_width] + qv_bias[:model_width]).astype(jnp.bfloat16)
    key_rows = projected[:, model_width : 2 * model_width].astype(jnp.bfloat16)
    value_rows = (projected[:, 2 * model_width :] + qv_bias[model_width:]).astype(jnp.bfloat16)
    query_heads = split_heads(queries)
    key_heads = split_heads(key_rows)
    value_heads = split_heads(value_rows)
    scores = (
        jnp.einsum(
            "sqhd,skhd->shqk", query_heads, key_heads, preferred_element_type=jnp.float32
        )
        * score_scale
    )
    highest_score = jnp.max(scores, -1, keepdims=True)
    exponent = jnp.exp(scores - highest_score)
    total_exp = jnp.sum(exponent, -1, keepdims=True)
    attn_probs = exponent / total_exp
    log_total = highest_score + jnp.log(total_exp)
    attended = jnp.einsum(
        "shqk,skhd->sqhd",
        attn_probs.astype(jnp.bfloat16),
        value_heads,
        preferred_element_type=jnp.float32,
    )
    attended = attended.reshape(rows, model_width).astype(jnp.bfloat16)
    hidden = source + matmul(attended, whole_attn) + bias_attn
    normed_two, unit_two, inv_two = norm_parts(hidden, gain_two, shift_two)
    normed_two_low = normed_two.astype(jnp.bfloat16)
    pre_act = matmul(normed_two_low, whole_up) + bias_up
    activated, derivative = gelu_parts(pre_act)
    act_low = activated.astype(jnp.bfloat16)
    result = hidden + matmul(act_low, whole_down) + bias_down
    block_out = (
        (result * live_rows).astype(jnp.bfloat16).reshape(slot_count, length, model_width)
    )
    grad_out = (
        cotangent[0, start : start + slot_count].reshape(rows, model_width).astype(jnp.float32)
        * live_rows
    )
    grad_out_low = grad_out.astype(jnp.bfloat16)
    grad_down = outer_sum(act_low, grad_out_low)
    grad_bias_down = jnp.sum(grad_out, 0)
    grad_pre = (times_rows(grad_out_low, whole_down) * derivative).astype(jnp.bfloat16)
    grad_up = outer_sum(normed_two_low, grad_pre)
    grad_bias_up = jnp.sum(grad_pre.astype(jnp.float32), 0)
    grad_normed_two = times_rows(grad_pre, whole_up)
    grad_gain_two = jnp.sum(grad_normed_two * unit_two, 0)
    grad_shift_two = jnp.sum(grad_normed_two, 0)
    grad_hidden = grad_out + norm_back(grad_normed_two, unit_two, inv_two, gain_two)
    grad_branch = grad_hidden.astype(jnp.bfloat16)
    grad_attn = outer_sum(attended, grad_branch)
    grad_bias_attn = jnp.sum(grad_branch.astype(jnp.float32), 0)
    grad_attended = split_heads(times_rows(grad_branch, whole_attn).astype(jnp.bfloat16))
    again = (
        jnp.einsum(
            "sqhd,skhd->shqk", query_heads, key_heads, preferred_element_type=jnp.float32
        )
        * score_scale
    )
    probs_again = jnp.exp(again - log_total)
    grad_values = jnp.einsum(
        "shqk,sqhd->skhd",
        probs_again.astype(jnp.bfloat16),
        grad_attended,
        preferred_element_type=jnp.float32,
    ).astype(jnp.bfloat16)
    grad_probs = jnp.einsum(
        "sqhd,skhd->shqk", grad_attended, value_heads, preferred_element_type=jnp.float32
    )
    row_dot = jnp.sum(grad_probs * probs_again, -1, keepdims=True)
    grad_scores = (probs_again * (grad_probs - row_dot)).astype(jnp.bfloat16)
    grad_queries = (
        jnp.einsum(
            "shqk,skhd->sqhd", grad_scores, key_heads, preferred_element_type=jnp.float32
        )
        * score_scale
    ).astype(jnp.bfloat16)
    grad_keys = (
        jnp.einsum(
            "shqk,sqhd->skhd", grad_scores, query_heads, preferred_element_type=jnp.float32
        )
        * score_scale
    ).astype(jnp.bfloat16)
    grad_qkv = jnp.concatenate(
        [
            grad_queries.reshape(rows, model_width),
            grad_keys.reshape(rows, model_width),
            grad_values.reshape(rows, model_width),
        ],
        axis=1,
    )
    grad_whole_qkv = outer_sum(normed_low, grad_qkv)
    grad_qv_bias = jnp.concatenate(
        [
            jnp.sum(grad_qkv[:, :model_width].astype(jnp.float32), 0),
            jnp.sum(grad_qkv[:, 2 * model_width :].astype(jnp.float32), 0),
        ]
    )
    grad_normed_one = times_rows(grad_qkv, whole_qkv)
    grad_gain_one = jnp.sum(grad_normed_one * unit_one, 0)
    grad_shift_one = jnp.sum(grad_normed_one, 0)
    grad_source = grad_hidden + norm_back(grad_normed_one, unit_one, inv_one, gain_one)
    grad_images = (
        grad_source.astype(jnp.bfloat16).reshape(slot_count, length, model_width)
    )
    grads = (
        grad_gain_one,
        grad_shift_one,
        grad_whole_qkv,
        grad_qv_bias,
        grad_attn,
        grad_bias_attn,
        grad_gain_two,
        grad_shift_two,
        grad_up,
        grad_bias_up,
        grad_down,
        grad_bias_down,
    )
    vectors = (0, 1, 3, 5, 6, 7, 9, 11)
    flat = jnp.concatenate([grads[k] for k in vectors])
    length_all = flat.shape[0]
    flat = jnp.pad(flat, (0, -length_all % 1024)).reshape(8, -1)
    flat = sum_everywhere(flat, inner, outer).reshape(-1)
    summed = {}
    at = 0
    for k in vectors:
        rows_here = grads[k].shape[0]
        part = rows_here // inner
        summed[k] = lax.dynamic_slice_in_dim(
            flat[at : at + rows_here], lax.axis_index("inner") * part, part, 0
        )
        at += rows_here
    for k in (10, 8, 4, 2):
        summed[k] = sum_to_owner(grads[k], inner, outer)
    return (block_out[None], grad_images[None]) + tuple(summed[k] for k in range(12))


def solution(mesh):
    return jax.shard_map(
        functools.partial(per_device, mesh.shape["inner"], mesh.shape["outer"]),
        mesh=mesh,
        in_specs=(
            P(("inner", "outer"), None, None, None),
            P(("inner", "outer")),
            P("inner"),
            P("inner"),
            P("inner", None),
            P("inner"),
            P("inner", None),
            P("inner"),
            P("inner"),
            P("inner"),
            P("inner", None),
            P("inner"),
            P("inner", None),
            P("inner"),
            P(("inner", "outer"), None, None, None),
        ),
        out_specs=(
            P(("inner", "outer"), None, None, None),
            P(("inner", "outer"), None, None, None),
            P("inner"),
            P("inner"),
            P("inner", None),
            P("inner"),
            P("inner", None),
            P("inner"),
            P("inner"),
            P("inner"),
            P("inner", None),
            P("inner"),
            P("inner", None),
            P("inner"),
        ),
        check_vma=False,
    )
```
